128 devices in a mesh: sec: 16 (over y, z_lo, core), head: 8 (over z_hi, x).
Axes of the slice: x: 4, y: 4, z: 4 (z_hi: 2, z_lo: 2; z = z_hi * 2 + z_lo), core: 2. Of those that a mesh axis runs over, the one named last changes fastest.
Arguments:
- tokens: bfloat16 [16384, 4096], P('sec')
- w_query: bfloat16 [4096, 4096], P(None, 'head')
- w_key: bfloat16 [4096, 1024], P(None, 'head')
- w_value: bfloat16 [4096, 1024], P(None, 'head'), may hold values from -0.09375 to 0.09375
- w_out: bfloat16 [4096, 4096], P('head'), may hold values from -0.375 to 0.375
- key_start: int32 [64], replicated, may hold values from 0 to 16128, as said below
Outputs:
- mixed: bfloat16 [16384, 4096], P('sec', 'head')
The draws below stay inside these ranges and needn't reach their ends.
Inputs may be any that keep to these rules, and one draw needn't show every extreme that they name: key_start[c] is a multiple of 256 and at most c * 256; the last block's entry is (64 - 1) * 256.
All inputs are finite; a program needn't handle non-finite values.
Results may differ from the reference program's by a relative error of at most 0.015.
The reference program's roundings to bfloat16 on the way count: a program that leaves them out, or rounds other values in their place, can miss the bound.
Values may be sent and summed in bfloat16 or wider, within the bound.
A program may use at most 128 MiB of HBM per device.

```python
import math
import jax
import jax.numpy as jnp
from jax import lax

D = 4096
QH = 32
KVH = 8
HD = 128
SPAN = 256
TOKENS = 16384
NCHUNK = 64
N_HEAD = 8


def shared_query(key):
    base = jax.random.normal(jax.random.fold_in(key, 7), (D, QH * HD), jnp.float32)
    return jnp.clip(base, -6.0, 6.0) * D ** (-0.5)


def draw_tokens(key, part):
    values = jnp.clip(jax.random.normal(jax.random.fold_in(key, 1), (TOKENS, D), jnp.float32), -6.0, 6.0)
    return values.astype(jnp.bfloat16)


def draw_w_query(key, part):
    base = shared_query(key)
    return base.astype(jnp.bfloat16)


def draw_w_key(key, part):
    fresh = jax.random.normal(jax.random.fold_in(key, 9), (D, KVH * HD), jnp.float32)
    return (jnp.clip(fresh, -6.0, 6.0) * D ** (-0.5)).astype(jnp.bfloat16)


def draw_key_start(key, part):
    index = jnp.arange(NCHUNK, dtype=jnp.int32)
    drawn = jax.random.randint(jax.random.fold_in(key, 5), (NCHUNK,), 0, index + 1, dtype=jnp.int32)
    drawn = jnp.where(index == NCHUNK - 1, NCHUNK - 1, drawn)
    return drawn * SPAN


def levels(rng, dims, pieces, low, top_value):
    level, own = 1.0, jax.random.fold_in(rng, 6)
    for dim, blocks in pieces:
        heights = jnp.exp(jax.random.uniform(jax.random.fold_in(own, dim), (blocks,), jnp.float32, low / len(pieces), top_value / len(pieces)))
        level = level * jnp.repeat(heights, dims[dim] // blocks).reshape([-1 if axis == dim else 1 for axis in range(len(dims))])
    return level


def noise(own_key, extent, deviation, reach, cuts=(), kind=jnp.bfloat16):
    values = deviation * jax.random.normal(own_key, extent, jnp.float32)
    if cuts:
        values = values * levels(own_key, extent, cuts, -0.22, 0.18)
    return jnp.clip(values, -reach, reach).astype(kind)


def setup_inputs(seed: int = 0) -> dict:
    arg_keys = jax.random.split(jax.random.key(seed), 7)
    return {
        "tokens": draw_tokens(jax.random.fold_in(arg_keys[6], 71), 0),
        "w_query": draw_w_query(jax.random.fold_in(arg_keys[6], 71), 0),
        "w_key": draw_w_key(jax.random.fold_in(arg_keys[6], 71), 0),
        "w_value": noise(arg_keys[3], (D, KVH * HD), D ** -0.5, 0.09375, ((1, 8),)),
        "w_out": noise(arg_keys[4], (QH * HD, D), (2 * HD) ** -0.5, 0.375, ((0, 8),)),
        "key_start": draw_key_start(jax.random.fold_in(arg_keys[6], 71), 0),
    }


def rotate(heads_data, position):
    midway = heads_data.shape[-1] // 2
    frequency = jnp.float32(500000.0) ** (-(jnp.arange(midway, dtype=jnp.float32) * 2.0) / heads_data.shape[-1])
    angle = position.astype(jnp.float32)[:, None] * frequency[None, :]
    cosine = jnp.cos(angle)[:, None, :]
    sine = jnp.sin(angle)[:, None, :]
    first_half = heads_data[..., :midway]
    second_half = heads_data[..., midway:]
    return jnp.concatenate([first_half * cosine - second_half * sine, second_half * cosine + first_half * sine], axis=-1)


def reference(tokens, w_query, w_key, w_value, w_out, key_start):
    total = tokens.shape[0]
    groups = QH // KVH
    position = jnp.arange(total, dtype=jnp.int32)
    query = rotate(jnp.dot(tokens, w_query, preferred_element_type=jnp.float32).reshape(total, QH, HD), position).astype(jnp.bfloat16)
    keys = rotate(jnp.dot(tokens, w_key, preferred_element_type=jnp.float32).reshape(total, KVH, HD), position).astype(jnp.bfloat16)
    values = jnp.dot(tokens, w_value, preferred_element_type=jnp.float32).astype(jnp.bfloat16).reshape(total, KVH, HD)
    visible_from = jnp.repeat(key_start, SPAN)
    block = math.gcd(total, 1024)
    scale = HD ** -0.5
    outputs = []
    for index in range(total // block):
        start = index * block
        finish = start + block
        query_block = query[start:finish].reshape(block, KVH, groups, HD).transpose(1, 2, 0, 3).astype(jnp.float32)
        key_block = keys[:finish].transpose(1, 0, 2).astype(jnp.float32)
        value_block = values[:finish].transpose(1, 0, 2).astype(jnp.float32)
        query_position = position[start:finish]
        lower = visible_from[start:finish]
        key_position = position[:finish]
        allowed = (key_position[None, :] >= lower[:, None]) & (key_position[None, :] <= query_position[:, None])

        def per_group(operands):
            query_group, key_group, value_group = operands
            scores = jnp.einsum('gqd,jd->gqj', query_group, key_group) * scale
            scores = jnp.where(allowed[None], scores, -jnp.inf)
            largest = jnp.max(scores, axis=-1, keepdims=True)
            weights = jnp.exp(scores - largest)
            weight_sum = jnp.sum(weights, axis=-1, keepdims=True)
            rounded = lax.optimization_barrier(weights.astype(jnp.bfloat16)).astype(jnp.float32)
            return jnp.einsum('gqj,jd->gqd', rounded, value_group) / weight_sum

        result = lax.map(per_group, (query_block, key_block, value_block))
        outputs.append(result.transpose(2, 0, 1, 3).reshape(block, QH * HD).astype(jnp.bfloat16))
    attention = jnp.concatenate(outputs, axis=0)
    width = QH * HD // N_HEAD
    mixed = jnp.zeros((total, w_out.shape[1]), jnp.float32)
    for member in range(N_HEAD):
        term = jnp.dot(attention[:, member * width:(member + 1) * width], w_out[member * width:(member + 1) * width], preferred_element_type=jnp.float32)
        mixed = mixed + lax.optimization_barrier(term.astype(jnp.bfloat16)).astype(jnp.float32)
    return mixed.astype(jnp.bfloat16)
```

```python
import functools
import math

import jax
import jax.numpy as jnp
from jax import lax
from jax.experimental import pallas as pl
from jax.experimental.pallas import tpu as pltpu
from jax.sharding import PartitionSpec as P

QH = 32
KVH = 8
HD = 128
SPAN = 256
GROUPS = QH // KVH
NY, NZ, NX = 4, 2, 4
MESH = pl.DeviceIdType.MESH
F32 = jnp.float32
BF16 = jnp.bfloat16
FINE = 32
CHUNK = 512
NBUF = 4


def rope_tables(start, rows):
    coarse = start + FINE * jnp.arange(rows // FINE, dtype=jnp.int32)
    fine = jnp.arange(FINE, dtype=jnp.int32)
    position = jnp.concatenate([coarse, fine]).astype(F32)
    lane = jnp.arange(HD, dtype=jnp.int32) % (HD // 2)
    frequency = F32(500000.0) ** (-(lane.astype(F32) * 2.0) / HD)
    angle = position[:, None] * frequency[None, :]
    return jnp.cos(angle), jnp.sin(angle)


def rope(x, cos, sin):
    return x * cos + pltpu.roll(x, HD // 2, 1) * sin


def tile_tables(cos_ref, sin_ref, first, count, coarse_rows):
    fine_c = cos_ref[coarse_rows:, :]
    fine_s = sin_ref[coarse_rows:, :]
    lane = lax.broadcasted_iota(jnp.int32, (FINE, HD), 1)
    sign = jnp.where(lane < HD // 2, F32(-1.0), F32(1.0))
    cs, ss = [], []
    for g in range(count):
        c = cos_ref[pl.ds(first + g, 1), :]
        s = sin_ref[pl.ds(first + g, 1), :]
        cs.append(c * fine_c - s * fine_s)
        ss.append((s * fine_c + c * fine_s) * sign)
    return jnp.concatenate(cs, axis=0), jnp.concatenate(ss, axis=0)


def kv_kernel(coarse_rows, tok_ref, wk_ref, wv_ref, cos_ref, sin_ref, kv_ref):
    rows = tok_ref.shape[0]
    count = rows // FINE
    cos, sin = tile_tables(cos_ref, sin_ref, pl.program_id(0) * count, count, coarse_rows)
    tok = tok_ref[...]
    k = jnp.dot(tok, wk_ref[...], preferred_element_type=F32)
    kv_ref[:, :HD] = rope(k, cos, sin).astype(BF16)
    v = jnp.dot(tok, wv_ref[...], preferred_element_type=F32)
    kv_ref[:, HD:] = v.astype(BF16)


def q_kernel(coarse_rows, tok_ref, wq_ref, cos_ref, sin_ref, q_ref):
    rows = tok_ref.shape[0]
    count = rows // FINE
    cos, sin = tile_tables(cos_ref, sin_ref, pl.program_id(0) * count, count, coarse_rows)
    q = jnp.dot(tok_ref[...], wq_ref[...], preferred_element_type=F32)
    for h in range(q.shape[1] // HD):
        cols = slice(h * HD, (h + 1) * HD)
        q_ref[:, cols] = rope(q[:, cols], cos, sin).astype(BF16)


def project(body, tokens, weights, tables, width, tile=256):
    rows, depth = tokens.shape
    full = lambda a: pl.BlockSpec(a.shape, lambda i: (0, 0))
    flops = 2 * rows * depth * width
    return pl.pallas_call(
        functools.partial(body, tables[0].shape[0] - FINE),
        out_shape=jax.ShapeDtypeStruct((rows, width), BF16),
        grid=(rows // tile,),
        in_specs=[pl.BlockSpec((tile, depth), lambda i: (i, 0))]
        + [full(a) for a in (*weights, *tables)],
        out_specs=pl.BlockSpec((tile, width), lambda i: (i, 0)),
        cost_estimate=pl.CostEstimate(
            flops=flops, bytes_accessed=2 * depth * (rows + width), transcendentals=0
        ),
    )(tokens, *weights, *tables)


def gather_kernel(own_ref, out_ref, send_sem, recv_sem, half_sem, own_sem):
    sec = lax.axis_index("sec")
    head = lax.axis_index("head")
    y = sec // 4
    z = (sec // 2) % 2
    c = sec % 2

    def at(yy, zz, cc):
        return (yy % NY) * 4 + zz * 2 + cc

    up, down = at(y + 1, z, c), at(y + 3, z, c)
    across, mate = at(y, 1 - z, c), at(y, z, 1 - c)
    barrier = pltpu.get_barrier_semaphore()
    for other in (up, down, across, mate):
        pl.semaphore_signal(barrier, inc=1, device_id=(other, head), device_id_type=MESH)
    pl.semaphore_wait(barrier, 4)

    rows = own_ref.shape[0]
    half = rows // 2
    sent = []

    def push(src, slot, part, target, sem):
        dst = out_ref.at[slot] if part is None else out_ref.at[slot, pl.ds(part * half, half)]
        copy = pltpu.make_async_remote_copy(
            src_ref=src,
            dst_ref=dst,
            send_sem=send_sem.at[len(sent)],
            recv_sem=sem,
            device_id=(target, head),
            device_id_type=MESH,
        )
        copy.start()
        sent.append(copy)

    def relay(slot, target):
        push(out_ref.at[slot], slot, None, target, recv_sem.at[slot])

    def arrived(slot):
        pltpu.make_async_copy(out_ref.at[slot], out_ref.at[slot], recv_sem.at[slot]).wait()

    def half_arrived(slot, part):
        view = out_ref.at[slot, pl.ds(part * half, half)]
        pltpu.make_async_copy(view, view, half_sem.at[part]).wait()

    keep = pltpu.make_async_copy(own_ref, out_ref.at[sec], own_sem)
    keep.start()
    for other in (up, down, across, mate):
        push(own_ref, sec, None, other, recv_sem.at[sec])
    far = at(y + 2, z, c)
    arrived(down)
    push(out_ref.at[down, pl.ds(0, half)], down, 0, up, half_sem.at[0])
    relay(down, mate)
    arrived(up)
    push(out_ref.at[up, pl.ds(half, half)], up, 1, down, half_sem.at[1])
    relay(up, mate)
    arrived(across)
    relay(across, up)
    relay(across, down)
    relay(across, mate)
    half_arrived(far, 0)
    half_arrived(far, 1)
    relay(far, across)
    relay(far, mate)
    for slot in (at(y + 1, 1 - z, c), at(y + 3, 1 - z, c), at(y + 2, 1 - z, c)):
        arrived(slot)
        relay(slot, mate)
    for yy in range(NY):
        for zz in range(NZ):
            arrived(at(yy, zz, 1 - c))
    keep.wait()
    for copy in sent:
        copy.wait_send()


def gather_kv(own, sections):
    rows, width = own.shape
    return pl.pallas_call(
        gather_kernel,
        out_shape=jax.ShapeDtypeStruct((sections, rows, width), own.dtype),
        in_specs=[pl.BlockSpec(memory_space=pltpu.VMEM)],
        out_specs=pl.BlockSpec(memory_space=pl.ANY),
        scratch_shapes=[
            pltpu.SemaphoreType.DMA((16,)),
            pltpu.SemaphoreType.DMA((16,)),
            pltpu.SemaphoreType.DMA((2,)),
            pltpu.SemaphoreType.DMA,
        ],
        compiler_params=pltpu.CompilerParams(collective_id=0, has_side_effects=True),
    )(own)


def attend_kernel(first, starts_ref, q_ref, kv_ref, o_ref, ring, edge, ring_sem, edge_sem, m_ref, l_ref, a_ref):
    block = lax.axis_index("sec") * (q_ref.shape[0] * 4 // SPAN) + first
    low = starts_ref[block] // SPAN
    number = block + 1 - low
    even = lax.rem(number, 2) == 0
    pairs = (number - 1) // 2
    factor = F32(HD**-0.5 * math.log2(math.e))

    def fetch(t):
        start = pl.multiple_of(low * SPAN + t * CHUNK, SPAN)
        slot = lax.rem(t, NBUF)
        return pltpu.make_async_copy(kv_ref.at[pl.ds(start, CHUNK)], ring.at[slot], ring_sem.at[slot])

    def fetch_edge(part):
        start = pl.multiple_of(jnp.maximum(block - 1 + part, 0) * SPAN, SPAN)
        return pltpu.make_async_copy(
            kv_ref.at[pl.ds(start, SPAN)], edge.at[pl.ds(part * SPAN, SPAN)], edge_sem.at[part]
        )

    fetch_edge(1).start()
    fetch_edge(0).start()
    for t in range(NBUF - 1):

        @pl.when(t < pairs)
        def _():
            fetch(t).start()

    def scores(h, keys):
        return lax.dot_general(
            q_ref[:, h * HD : (h + 1) * HD], keys, (((1,), (1,)), ((), ())), preferred_element_type=F32
        )

    def weigh(s, top, width):
        parts = [jnp.exp2((s[:, g * HD : (g + 1) * HD] - top) * factor) for g in range(width // HD)]
        total = functools.reduce(lambda a, b: a + b, parts)
        return jnp.concatenate([p.astype(BF16) for p in parts], axis=1), total

    def begin(width):
        keys = edge[2 * SPAN - width :, :HD]
        values = edge[2 * SPAN - width :, HD:]
        row = lax.broadcasted_iota(jnp.int32, (SPAN, width), 0)
        col = lax.broadcasted_iota(jnp.int32, (SPAN, width), 1) - (width - SPAN)
        for h in range(GROUPS):
            s = jnp.where(col <= row, scores(h, keys), -jnp.inf)
            top = jnp.broadcast_to(jnp.max(s, axis=1, keepdims=True), (SPAN, HD))
            p, total = weigh(s, top, width)
            m_ref[h] = top
            l_ref[h] = total
            a_ref[h] = jnp.dot(p, values, preferred_element_type=F32)

    fetch_edge(1).wait()
    fetch_edge(0).wait()

    @pl.when(even)
    def _():
        begin(2 * SPAN)

    @pl.when(jnp.logical_not(even))
    def _():
        begin(SPAN)

    @pl.loop(0, pairs)
    def _(t):
        @pl.when(t + NBUF - 1 < pairs)
        def _():
            fetch(t + NBUF - 1).start()

        fetch(t).wait()
        slot = lax.rem(t, NBUF)
        keys = ring[slot, :, :HD]
        values = ring[slot, :, HD:]
        for h in range(GROUPS):
            s = scores(h, keys)
            old = m_ref[h]
            top = jnp.maximum(old, jnp.max(s, axis=1, keepdims=True))
            scale = jnp.exp2((old - top) * factor)
            p, total = weigh(s, top, CHUNK)
            m_ref[h] = top
            l_ref[h] = l_ref[h] * scale + total
            a_ref[h] = a_ref[h] * scale + jnp.dot(p, values, preferred_element_type=F32)

    for h in range(GROUPS):
        weight = jnp.sum(l_ref[h], axis=1, keepdims=True)
        o_ref[:, h * HD : (h + 1) * HD] = (a_ref[h] / weight).astype(BF16)


def attend(first, starts, query, kv):
    rows, width = query.shape
    state = pltpu.VMEM((GROUPS, SPAN, HD), F32)
    pairs = 40
    return pl.pallas_call(
        functools.partial(attend_kernel, first),
        out_shape=jax.ShapeDtypeStruct((SPAN, width), BF16),
        grid_spec=pltpu.PrefetchScalarGridSpec(
            num_scalar_prefetch=1,
            grid=(1,),
            in_specs=[
                pl.BlockSpec((SPAN, width), lambda i, s: (first, 0)),
                pl.BlockSpec(memory_space=pl.ANY),
            ],
            out_specs=pl.BlockSpec((SPAN, width), lambda i, s: (0, 0)),
            scratch_shapes=[
                pltpu.VMEM((NBUF, CHUNK, 2 * HD), BF16),
                pltpu.VMEM((2 * SPAN, 2 * HD), BF16),
                pltpu.SemaphoreType.DMA((NBUF,)),
                pltpu.SemaphoreType.DMA((2,)),
                state,
                state,
                state,
            ],
        ),
        cost_estimate=pl.CostEstimate(
            flops=pairs * 8 * SPAN * SPAN * HD * GROUPS,
            bytes_accessed=pairs * SPAN * 4 * HD,
            transcendentals=pairs * SPAN * SPAN * GROUPS,
        ),
        name="attend",
    )(starts, query, kv)


def output_kernel(a0, a1, a2, a3, w_ref, keep_ref, give_ref):
    half = keep_ref.shape[1]
    for part, ref in ((0, keep_ref), (1, give_ref)):
        cols = slice(part * half, (part + 1) * half)
        total = None
        for r, att in enumerate((a0, a1, a2, a3)):
            term = jnp.dot(att[...], w_ref[r, :, cols], preferred_element_type=F32)
            term = term.astype(BF16).astype(F32)
            total = term if total is None else total + term
        ref[...] = total.astype(ref.dtype)


def output(pieces, weights):
    rows, depth = pieces[0].shape
    cols = weights.shape[2] // 2
    return pl.pallas_call(
        output_kernel,
        out_shape=(
            jax.ShapeDtypeStruct((rows, cols), F32),
            jax.ShapeDtypeStruct((rows, cols), BF16),
        ),
        cost_estimate=pl.CostEstimate(
            flops=16 * rows * depth * cols,
            bytes_accessed=2 * (4 * rows * depth + 8 * depth * cols),
            transcendentals=0,
        ),
        name="output",
    )(*pieces, weights)


def shards(tokens, w_query, w_key, w_value, w_out, key_start):
    rows = tokens.shape[0]
    sections = lax.axis_size("sec")
    section = lax.axis_index("sec")
    head = lax.axis_index("head")
    x, z = head % NX, head // NX
    ring = lambda step: [(zz * NX + xx, zz * NX + (xx + step) % NX) for zz in range(2) for xx in range(NX)]
    swap = [(h, (h + NX) % (2 * NX)) for h in range(2 * NX)]

    depth = w_out.shape[0]
    cols = w_out.shape[1] // (2 * NX)

    def piece(r):
        target = (x - r) % NX
        mine = lax.dynamic_slice(w_out, (0, (z * NX + target) * cols), (depth, cols))
        other = lax.dynamic_slice(w_out, (0, ((1 - z) * NX + target) * cols), (depth, cols))
        return jnp.concatenate([mine, other], axis=1)

    weights = [piece(0)] + [lax.ppermute(piece(r), "head", ring(-r)) for r in range(1, NX)]
    weights = jnp.stack(weights)

    tables = rope_tables(section * rows, rows)
    own = project(kv_kernel, tokens, (w_key, w_value), tables, 2 * HD)
    kv = gather_kv(own, sections).reshape(sections * rows, 2 * HD)
    query = project(q_kernel, tokens, (w_query,), tables, GROUPS * HD)

    done = []
    for i in range(rows // SPAN):
        att = attend(i, key_start, query, kv)
        pieces = [att] + [lax.ppermute(att, "head", ring(-r)) for r in range(1, NX)]
        keep, give = output(pieces, weights)
        got = lax.ppermute(give, "head", swap)
        done.append((keep + got.astype(F32)).astype(BF16))
    return jnp.concatenate(done, axis=0)


def solution(mesh):
    placed = (
        P("sec", None),
        P(None, "head"),
        P(None, "head"),
        P(None, "head"),
        P("head", None),
        P(),
    )
    return jax.shard_map(
        shards, mesh=mesh, in_specs=placed, out_specs=P("sec", "head"), check_vma=False
    )
```

```python
import functools
import math

import jax
import jax.numpy as jnp
from jax import lax
from jax.experimental import pallas as pl
from jax.experimental.pallas import tpu as pltpu
from jax.sharding import PartitionSpec as P

QH = 32
KVH = 8
HD = 128
SPAN = 256
GROUPS = QH // KVH
NY, NZ, NX = 4, 2, 4
MESH = pl.DeviceIdType.MESH
F32 = jnp.float32
BF16 = jnp.bfloat16
FINE = 32
CHUNK = 512
NBUF = 4


def rope_tables(start, rows):
    coarse = start + FINE * jnp.arange(rows // FINE, dtype=jnp.int32)
    fine = jnp.arange(FINE, dtype=jnp.int32)
    position = jnp.concatenate([coarse, fine]).astype(F32)
    lane = jnp.arange(HD, dtype=jnp.int32) % (HD // 2)
    frequency = F32(500000.0) ** (-(lane.astype(F32) * 2.0) / HD)
    angle = position[:, None] * frequency[None, :]
    return jnp.cos(angle), jnp.sin(angle)


def rope(x, cos, sin):
    return x * cos + pltpu.roll(x, HD // 2, 1) * sin


def tile_tables(cos_ref, sin_ref, first, count, coarse_rows):
    fine_c = cos_ref[coarse_rows:, :]
    fine_s = sin_ref[coarse_rows:, :]
    lane = lax.broadcasted_iota(jnp.int32, (FINE, HD), 1)
    sign = jnp.where(lane < HD // 2, F32(-1.0), F32(1.0))
    cs, ss = [], []
    for g in range(count):
        c = cos_ref[pl.ds(first + g, 1), :]
        s = sin_ref[pl.ds(first + g, 1), :]
        cs.append(c * fine_c - s * fine_s)
        ss.append((s * fine_c + c * fine_s) * sign)
    return jnp.concatenate(cs, axis=0), jnp.concatenate(ss, axis=0)


def kv_kernel(coarse_rows, tok_ref, wk_ref, wv_ref, cos_ref, sin_ref, kv_ref):
    rows = tok_ref.shape[0]
    count = rows // FINE
    cos, sin = tile_tables(cos_ref, sin_ref, pl.program_id(0) * count, count, coarse_rows)
    weights = jnp.concatenate([wk_ref[...], wv_ref[...]], axis=1)
    kv = jnp.dot(tok_ref[...], weights, preferred_element_type=F32)
    kv_ref[:, :HD] = rope(kv[:, :HD], cos, sin).astype(BF16)
    kv_ref[:, HD:] = kv[:, HD:].astype(BF16)


def project(body, tokens, weights, tables, width, tile=256):
    rows, depth = tokens.shape
    full = lambda a: pl.BlockSpec(a.shape, lambda i: (0, 0))
    flops = 2 * rows * depth * width
    return pl.pallas_call(
        functools.partial(body, tables[0].shape[0] - FINE),
        out_shape=jax.ShapeDtypeStruct((rows, width), BF16),
        grid=(rows // tile,),
        in_specs=[pl.BlockSpec((tile, depth), lambda i: (i, 0))]
        + [full(a) for a in (*weights, *tables)],
        out_specs=pl.BlockSpec((tile, width), lambda i: (i, 0)),
        cost_estimate=pl.CostEstimate(
            flops=flops, bytes_accessed=2 * depth * (rows + width), transcendentals=0
        ),
    )(tokens, *weights, *tables)


def gather_kernel(
    own_ref, tok_ref, wq_ref, wo_ref, cos_ref, sin_ref, out_ref, w_ref, q_ref,
    tok_buf, wq_buf, send_sem, recv_sem, half_sem, own_sem, tok_sem, wq_sem, ws_sem, wr_sem, wm_sem,
):
    sec = lax.axis_index("sec")
    head = lax.axis_index("head")
    y = sec // 4
    z = (sec // 2) % 2
    c = sec % 2
    x, deep = head % NX, head // NX

    def at(yy, zz, cc):
        return (yy % NY) * 4 + zz * 2 + cc

    up, down = at(y + 1, z, c), at(y + 3, z, c)
    across, mate = at(y, 1 - z, c), at(y, z, 1 - c)
    chunk = tok_buf.shape[1]
    chunks = tok_ref.shape[0] // chunk

    def load(i):
        return pltpu.make_async_copy(
            tok_ref.at[pl.ds(i * chunk, chunk)], tok_buf.at[i % 2], tok_sem.at[i % 2]
        )

    load_wq = pltpu.make_async_copy(wq_ref, wq_buf, wq_sem)
    load_wq.start()
    load(0).start()
    barrier = pltpu.get_barrier_semaphore()
    for other in (up, down, across, mate):
        pl.semaphore_signal(barrier, inc=1, device_id=(other, head), device_id_type=MESH)
    for r in range(1, NX):
        other = deep * NX + (x + r) % NX
        pl.semaphore_signal(barrier, inc=1, device_id=(sec, other), device_id_type=MESH)
    pl.semaphore_wait(barrier, 3 + NX)

    rows = own_ref.shape[0]
    half = rows // 2
    sent = []

    def push(src, slot, part, target, sem):
        dst = out_ref.at[slot] if part is None else out_ref.at[slot, pl.ds(part * half, half)]
        copy = pltpu.make_async_remote_copy(
            src_ref=src,
            dst_ref=dst,
            send_sem=send_sem.at[len(sent)],
            recv_sem=sem,
            device_id=(target, head),
            device_id_type=MESH,
        )
        copy.start()
        sent.append(copy)

    def relay(slot, target):
        push(out_ref.at[slot], slot, None, target, recv_sem.at[slot])

    def arrived(slot):
        pltpu.make_async_copy(out_ref.at[slot], out_ref.at[slot], recv_sem.at[slot]).wait()

    def half_arrived(slot, part):
        view = out_ref.at[slot, pl.ds(part * half, half)]
        pltpu.make_async_copy(view, view, half_sem.at[part]).wait()

    keep = pltpu.make_async_copy(own_ref, out_ref.at[sec], own_sem)
    keep.start()
    for other in (up, down, across, mate):
        push(own_ref, sec, None, other, recv_sem.at[sec])

    cols = wo_ref.shape[1] // (2 * NX)
    part_rows = pl.ds(c * (wo_ref.shape[0] // 2), wo_ref.shape[0] // 2)

    def give(r, side):
        target = (x + NX - r) % NX
        first = pl.multiple_of(((deep + side) % 2 * NX + target) * cols, cols)
        return pltpu.make_async_remote_copy(
            src_ref=wo_ref.at[part_rows, pl.ds(first, cols)],
            dst_ref=w_ref.at[r - 1, part_rows, pl.ds(side * cols, cols)],
            send_sem=ws_sem.at[r - 1, side],
            recv_sem=wr_sem.at[r - 1, side],
            device_id=(sec, deep * NX + target),
            device_id_type=MESH,
        )

    def share(r):
        view = w_ref.at[r - 1, part_rows]
        return pltpu.make_async_remote_copy(
            src_ref=view,
            dst_ref=view,
            send_sem=wm_sem.at[0, r - 1],
            recv_sem=wm_sem.at[1, r - 1],
            device_id=(mate, head),
            device_id_type=MESH,
        )

    for r in range(1, NX):
        for side in range(2):
            give(r, side).start()

    coarse_rows = cos_ref.shape[0] - FINE
    load_wq.wait()
    for i in range(chunks):
        if i + 1 < chunks:
            load(i + 1).start()
        load(i).wait()
        cos, sin = tile_tables(cos_ref, sin_ref, i * (chunk // FINE), chunk // FINE, coarse_rows)
        q = jnp.dot(tok_buf[i % 2], wq_buf[...], preferred_element_type=F32)
        for h in range(GROUPS):
            cut = slice(h * HD, (h + 1) * HD)
            q_ref[i * chunk : (i + 1) * chunk, cut] = rope(q[:, cut], cos, sin).astype(BF16)

    far = at(y + 2, z, c)
    arrived(down)
    push(out_ref.at[down, pl.ds(0, half)], down, 0, up, half_sem.at[0])
    relay(down, mate)
    arrived(up)
    push(out_ref.at[up, pl.ds(half, half)], up, 1, down, half_sem.at[1])
    relay(up, mate)
    arrived(across)
    relay(across, up)
    relay(across, down)
    relay(across, mate)
    half_arrived(far, 0)
    half_arrived(far, 1)
    relay(far, across)
    relay(far, mate)
    for r in range(1, NX):
        for side in range(2):
            give(r, side).wait_recv()
        share(r).start()
    for slot in (at(y + 1, 1 - z, c), at(y + 3, 1 - z, c), at(y + 2, 1 - z, c)):
        arrived(slot)
        relay(slot, mate)
    for yy in range(NY):
        for zz in range(NZ):
            arrived(at(yy, zz, 1 - c))
    view = w_ref.at[0, pl.ds((1 - c) * (wo_ref.shape[0] // 2), wo_ref.shape[0] // 2)]
    for r in range(1, NX):
        pltpu.make_async_copy(view, view, wm_sem.at[1, r - 1]).wait()
    keep.wait()
    for copy in sent:
        copy.wait_send()
    for r in range(1, NX):
        for side in range(2):
            give(r, side).wait_send()
        share(r).wait_send()


def gather(own, tokens, w_query, w_out, tables, sections):
    rows, width = own.shape
    depth, wide = w_query.shape
    hbm = pl.BlockSpec(memory_space=pl.ANY)
    vmem = pl.BlockSpec(memory_space=pltpu.VMEM)
    cols = w_out.shape[1] // NX
    dma = pltpu.SemaphoreType.DMA
    return pl.pallas_call(
        gather_kernel,
        out_shape=(
            jax.ShapeDtypeStruct((sections, rows, width), BF16),
            jax.ShapeDtypeStruct((NX - 1, w_out.shape[0], cols), BF16),
            jax.ShapeDtypeStruct((rows, wide), BF16),
        ),
        in_specs=[vmem, hbm, hbm, hbm, vmem, vmem],
        out_specs=(hbm, hbm, vmem),
        scratch_shapes=[
            pltpu.VMEM((2, 256, depth), BF16),
            pltpu.VMEM((depth, wide), BF16),
            dma((16,)),
            dma((16,)),
            dma((2,)),
            dma,
            dma((2,)),
            dma,
            dma((NX - 1, 2)),
            dma((NX - 1, 2)),
            dma((2, NX - 1)),
        ],
        compiler_params=pltpu.CompilerParams(collective_id=0, has_side_effects=True),
        name="gather",
    )(own, tokens, w_query, w_out, *tables)


def attend_kernel(
    starts_ref, q_ref, kv_ref, o_ref, ring, edge, s_buf, p_buf, f_buf, ring_sem, edge_sem, m_ref, l_ref, a_ref
):
    step = pl.program_id(0)
    blocks = pl.num_programs(0)
    block = lax.axis_index("sec") * blocks + step
    low = starts_ref[block] // SPAN
    number = block + 1 - low
    even = lax.rem(number, 2) == 0
    pairs = (number - 1) // 2
    factor = F32(HD**-0.5 * math.log2(math.e))

    def slot_of(t):
        return lax.rem(t + NBUF, NBUF)

    def fetch(t):
        start = pl.multiple_of(low * SPAN + t * CHUNK, SPAN)
        slot = slot_of(t)
        return pltpu.make_async_copy(kv_ref.at[pl.ds(start, CHUNK)], ring.at[slot], ring_sem.at[slot])

    def fetch_edge(part, rows):
        first = lax.axis_index("sec") * blocks
        start = pl.multiple_of((first if part else jnp.maximum(first - 1, 0)) * SPAN, SPAN)
        return pltpu.make_async_copy(
            kv_ref.at[pl.ds(start, rows)], edge.at[pl.ds(part * SPAN, rows)], edge_sem.at[part]
        )

    @pl.when(step == 0)
    def _():
        fetch_edge(1, edge.shape[0] - SPAN).start()
        fetch_edge(0, SPAN).start()

    for t in range(NBUF - 2):

        @pl.when(t < pairs)
        def _():
            fetch(t).start()

    @pl.when(step == 0)
    def _():
        ring[NBUF - 1] = jnp.zeros(ring.shape[1:], ring.dtype)
        fetch_edge(1, edge.shape[0] - SPAN).wait()
        fetch_edge(0, SPAN).wait()

    def scores(h, keys):
        return lax.dot_general(
            q_ref[:, h * HD : (h + 1) * HD], keys, (((1,), (1,)), ((), ())), preferred_element_type=F32
        )

    def weigh(s, top, width):
        parts = [jnp.exp2((s[:, g * HD : (g + 1) * HD] - top) * factor) for g in range(width // HD)]
        total = functools.reduce(lambda a, b: a + b, parts)
        return jnp.concatenate([p.astype(BF16) for p in parts], axis=1), total

    def begin(width):
        start = pl.multiple_of((step + 2) * SPAN - width, SPAN)
        keys = edge[pl.ds(start, width), :HD]
        values = edge[pl.ds(start, width), HD:]
        row = lax.broadcasted_iota(jnp.int32, (SPAN, width), 0)
        col = lax.broadcasted_iota(jnp.int32, (SPAN, width), 1) - (width - SPAN)
        for h in range(GROUPS):
            s = jnp.where(col <= row, scores(h, keys), -jnp.inf)
            top = jnp.broadcast_to(jnp.max(s, axis=1, keepdims=True), (SPAN, HD))
            p, total = weigh(s, top, width)
            m_ref[h] = top
            l_ref[h] = total
            a_ref[h] = jnp.dot(p, values, preferred_element_type=F32)

    @pl.when(even)
    def _():
        begin(2 * SPAN)

    @pl.when(jnp.logical_not(even))
    def _():
        begin(SPAN)

    p_buf[1] = jnp.zeros(p_buf.shape[1:], p_buf.dtype)
    f_buf[1] = jnp.ones(f_buf.shape[1:], f_buf.dtype)

    def gathered(h, half, values):
        a_ref[h] = a_ref[h] * f_buf[half] + jnp.dot(p_buf[half], values, preferred_element_type=F32)

    @pl.when(pairs > 0)
    def _():
        fetch(0).wait()
        s_buf[0] = scores(0, ring[0, :, :HD])

    @pl.loop(0, pairs)
    def _(t):
        @pl.when(t + 2 < pairs)
        def _():
            fetch(t + 2).start()

        @pl.when(t + 1 < pairs)
        def _():
            fetch(t + 1).wait()

        now, last, following = slot_of(t), slot_of(t - 1), slot_of(t + 1)
        for h in range(GROUPS):
            half = h % 2
            if h + 1 < GROUPS:
                s_buf[1 - half] = scores(h + 1, ring[now, :, :HD])
            else:
                s_buf[1 - half] = scores(0, ring[following, :, :HD])
            gathered((h - 1) % GROUPS, 1 - half, ring[now if h else last, :, HD:])
            s = s_buf[half]
            old = m_ref[h]
            top = jnp.maximum(old, jnp.max(s, axis=1, keepdims=True))
            scale = jnp.exp2((old - top) * factor)
            p, total = weigh(s, top, CHUNK)
            p_buf[half] = p
            f_buf[half] = scale
            m_ref[h] = top
            l_ref[h] = l_ref[h] * scale + total

    gathered(GROUPS - 1, 1, ring[slot_of(pairs - 1), :, HD:])
    for h in range(GROUPS):
        weight = jnp.sum(l_ref[h], axis=1, keepdims=True)
        o_ref[:, h * HD : (h + 1) * HD] = (a_ref[h] / weight).astype(BF16)


def attend(starts, query, kv):
    rows, width = query.shape
    state = pltpu.VMEM((GROUPS, SPAN, HD), F32)
    pairs = 120
    return pl.pallas_call(
        attend_kernel,
        out_shape=jax.ShapeDtypeStruct((rows, width), BF16),
        grid_spec=pltpu.PrefetchScalarGridSpec(
            num_scalar_prefetch=1,
            grid=(rows // SPAN,),
            in_specs=[
                pl.BlockSpec((SPAN, width), lambda i, s: (i, 0)),
                pl.BlockSpec(memory_space=pl.ANY),
            ],
            out_specs=pl.BlockSpec((SPAN, width), lambda i, s: (i, 0)),
            scratch_shapes=[
                pltpu.VMEM((NBUF, CHUNK, 2 * HD), BF16),
                pltpu.VMEM((rows + SPAN, 2 * HD), BF16),
                pltpu.VMEM((2, SPAN, CHUNK), F32),
                pltpu.VMEM((2, SPAN, CHUNK), BF16),
                pltpu.VMEM((2, SPAN, HD), F32),
                pltpu.SemaphoreType.DMA((NBUF,)),
                pltpu.SemaphoreType.DMA((2,)),
                state,
                state,
                state,
            ],
        ),
        cost_estimate=pl.CostEstimate(
            flops=pairs * 8 * SPAN * SPAN * HD * GROUPS,
            bytes_accessed=pairs * SPAN * 4 * HD,
            transcendentals=pairs * SPAN * SPAN * GROUPS,
        ),
        name="attend",
    )(starts, query, kv)


def output_kernel(
    att_ref, wo_ref, w_ref, o_ref, w_buf, near, keep, give, got, w_sem, own_send, own_recv, pass_send, pass_recv, swap_send, swap_recv
):
    sec = lax.axis_index("sec")
    head = lax.axis_index("head")
    x, deep = head % NX, head // NX
    up = deep * NX + (x + 1) % NX
    down = deep * NX + (x + NX - 1) % NX
    pair = (1 - deep) * NX + x
    count, chunk = own_send.shape[1], give.shape[1]
    half = chunk // 2
    cols = o_ref.shape[1]

    loads = [pltpu.make_async_copy(w_ref.at[r - 1], w_buf.at[r], w_sem.at[r + 1]) for r in range(1, NX)]
    for side in range(2):
        first = pl.multiple_of(((deep + side) % 2 * NX + x) * cols, cols)
        loads.append(
            pltpu.make_async_copy(
                wo_ref.at[:, pl.ds(first, cols)], w_buf.at[0, :, pl.ds(side * cols, cols)], w_sem.at[side]
            )
        )
    for load in loads:
        load.start()
    barrier = pltpu.get_barrier_semaphore()
    for other in (up, down, pair):
        pl.semaphore_signal(barrier, inc=1, device_id=(sec, other), device_id_type=MESH)
    pl.semaphore_wait(barrier, 3)

    def own(way, i):
        rows = pl.ds(pl.multiple_of(i * chunk, chunk), chunk)
        return pltpu.make_async_remote_copy(
            src_ref=att_ref.at[rows],
            dst_ref=near.at[0 if way else 2, rows],
            send_sem=own_send.at[way, i],
            recv_sem=own_recv.at[way, i],
            device_id=(sec, down if way else up),
            device_id_type=MESH,
        )

    def onward(way, i):
        rows = pl.ds(pl.multiple_of(i * chunk + (0 if way else half), half), half)
        return pltpu.make_async_remote_copy(
            src_ref=near.at[0 if way else 2, rows],
            dst_ref=near.at[1, rows],
            send_sem=pass_send.at[way, i],
            recv_sem=pass_recv.at[way, i],
            device_id=(sec, down if way else up),
            device_id_type=MESH,
        )

    def swap(i):
        return pltpu.make_async_remote_copy(
            src_ref=give.at[i],
            dst_ref=got.at[i],
            send_sem=swap_send.at[i],
            recv_sem=swap_recv.at[i],
            device_id=(sec, pair),
            device_id_type=MESH,
        )

    def product(i, side):
        rows = pl.ds(pl.multiple_of(i * chunk, chunk), chunk)
        total = None
        for r in range(NX):
            att = att_ref[rows, :] if r == 0 else near[r - 1, rows, :]
            term = jnp.dot(att, w_buf[r, :, side * cols : (side + 1) * cols], preferred_element_type=F32)
            term = term.astype(BF16).astype(F32)
            total = term if total is None else total + term
        return total

    for i in range(2):
        for way in range(2):
            own(way, i).start()
    for load in loads:
        load.wait()

    @pl.loop(0, count + 2)
    def _(i):
        @pl.when(i < count)
        def _():
            for way in range(2):
                own(way, i).wait_recv()
                onward(way, i).start()

        @pl.when(i + 2 < count)
        def _():
            for way in range(2):
                own(way, i + 2).start()

        @pl.when((i >= 1) & (i <= count))
        def _():
            j = i - 1
            for way in range(2):
                onward(way, j).wait_recv()
            give[j] = product(j, 1).astype(BF16)
            keep[lax.rem(j, 2)] = product(j, 0)
            swap(j).start()

        @pl.when(i >= 2)
        def _():
            j = i - 2
            swap(j).wait_recv()
            rows = pl.ds(pl.multiple_of(j * chunk, chunk), chunk)
            o_ref[rows, :] = (keep[lax.rem(j, 2)] + got[j].astype(F32)).astype(BF16)

    @pl.loop(0, count)
    def _(i):
        for way in range(2):
            own(way, i).wait_send()
            onward(way, i).wait_send()
        swap(i).wait_send()


def output(attended, w_out, w_near, chunk=128):
    rows, depth = attended.shape
    cols = w_out.shape[1] // (2 * NX)
    count = rows // chunk
    hbm = pl.BlockSpec(memory_space=pl.ANY)
    vmem = pl.BlockSpec(memory_space=pltpu.VMEM)
    dma = pltpu.SemaphoreType.DMA
    return pl.pallas_call(
        output_kernel,
        out_shape=jax.ShapeDtypeStruct((rows, cols), BF16),
        in_specs=[vmem, hbm, hbm],
        out_specs=vmem,
        scratch_shapes=[
            pltpu.VMEM((NX, depth, 2 * cols), BF16),
            pltpu.VMEM((NX - 1, rows, depth), BF16),
            pltpu.VMEM((2, chunk, cols), F32),
            pltpu.VMEM((count, chunk, cols), BF16),
            pltpu.VMEM((count, chunk, cols), BF16),
            dma((NX + 1,)),
            dma((2, count)),
            dma((2, count)),
            dma((2, count)),
            dma((2, count)),
            dma((count,)),
            dma((count,)),
        ],
        compiler_params=pltpu.CompilerParams(collective_id=1, has_side_effects=True),
        name="output",
    )(attended, w_out, w_near)


def shards(tokens, w_query, w_key, w_value, w_out, key_start):
    rows = tokens.shape[0]
    sections = lax.axis_size("sec")
    section = lax.axis_index("sec")
    tables = rope_tables(section * rows, rows)
    own = project(kv_kernel, tokens, (w_key, w_value), tables, 2 * HD)
    kv, w_near, query = gather(own, tokens, w_query, w_out, tables, sections)
    kv = kv.reshape(sections * rows, 2 * HD)
    attended = attend(key_start, query, kv)
    return output(attended, w_out, w_near)


def solution(mesh):
    placed = (
        P("sec", None),
        P(None, "head"),
        P(None, "head"),
        P(None, "head"),
        P("head", None),
        P(),
    )
    return jax.shard_map(
        shards, mesh=mesh, in_specs=placed, out_specs=P("sec", "head"), check_vma=False
    )
```

```python
import functools
import math

import jax
import jax.numpy as jnp
from jax import lax
from jax.experimental import pallas as pl
from jax.experimental.pallas import tpu as pltpu
from jax.sharding import PartitionSpec as P

QH = 32
KVH = 8
HD = 128
SPAN = 256
GROUPS = QH // KVH
NY, NZ, NX = 4, 2, 4
MESH = pl.DeviceIdType.MESH
F32 = jnp.float32
BF16 = jnp.bfloat16
FINE = 32
CHUNK = 512
NBUF = 4
BEHIND = 4
EARLY = 3
FACTOR = HD**-0.5 * math.log2(math.e)


def rope_tables(start, rows):
    coarse = start + FINE * jnp.arange(rows // FINE, dtype=jnp.int32)
    fine = jnp.arange(FINE, dtype=jnp.int32)
    position = jnp.concatenate([coarse, fine]).astype(F32)
    lane = jnp.arange(HD, dtype=jnp.int32) % (HD // 2)
    frequency = F32(500000.0) ** (-(lane.astype(F32) * 2.0) / HD)
    angle = position[:, None] * frequency[None, :]
    return jnp.cos(angle), jnp.sin(angle)


def rope(x, cos, sin):
    return x * cos + pltpu.roll(x, HD // 2, 1) * sin


def tile_tables(cos_ref, sin_ref, first, count, coarse_rows):
    fine_c = cos_ref[coarse_rows:, :]
    fine_s = sin_ref[coarse_rows:, :]
    lane = lax.broadcasted_iota(jnp.int32, (FINE, HD), 1)
    sign = jnp.where(lane < HD // 2, F32(-1.0), F32(1.0))
    cs, ss = [], []
    for g in range(count):
        c = cos_ref[pl.ds(first + g, 1), :]
        s = sin_ref[pl.ds(first + g, 1), :]
        cs.append(c * fine_c - s * fine_s)
        ss.append((s * fine_c + c * fine_s) * sign)
    return jnp.concatenate(cs, axis=0), jnp.concatenate(ss, axis=0)


def kv_kernel(coarse_rows, tok_ref, wk_ref, wv_ref, cos_ref, sin_ref, kv_ref, total):
    step = pl.program_id(0)
    weights = jnp.concatenate([wk_ref[...], wv_ref[...]], axis=1)
    term = jnp.dot(tok_ref[...], weights, preferred_element_type=F32)

    @pl.when(step == 0)
    def _():
        total[...] = term

    @pl.when(step > 0)
    def _():
        total[...] += term

    @pl.when(step == pl.num_programs(0) - 1)
    def _():
        cos, sin = tile_tables(cos_ref, sin_ref, 0, coarse_rows, coarse_rows)
        kv_ref[:, :HD] = rope(total[:, :HD], cos, sin).astype(BF16)
        kv_ref[:, HD:] = total[:, HD:].astype(BF16)


def project_kv(tokens, w_key, w_value, tables, tile=512):
    rows, depth = tokens.shape
    full = lambda a: pl.BlockSpec(a.shape, lambda i: (0, 0))
    weight = pl.BlockSpec((tile, HD), lambda i: (i, 0))
    return pl.pallas_call(
        functools.partial(kv_kernel, tables[0].shape[0] - FINE),
        out_shape=jax.ShapeDtypeStruct((rows, 2 * HD), BF16),
        grid=(depth // tile,),
        in_specs=[
            pl.BlockSpec((rows, tile), lambda i: (0, i)),
            weight,
            weight,
            full(tables[0]),
            full(tables[1]),
        ],
        out_specs=pl.BlockSpec((rows, 2 * HD), lambda i: (0, 0)),
        scratch_shapes=[pltpu.VMEM((rows, 2 * HD), F32)],
        name="project_kv",
    )(tokens, w_key, w_value, *tables)


def score(queries, keys):
    return lax.dot_general(queries, keys, (((1,), (1,)), ((), ())), preferred_element_type=F32)


def weigh(s, tops):
    parts = [jnp.exp2((s[:, g * HD : (g + 1) * HD] - top) * F32(FACTOR)) for g, top in enumerate(tops)]
    total = functools.reduce(lambda a, b: a + b, parts)
    return jnp.concatenate([p.astype(BF16) for p in parts], axis=1), total


def first_block(i, q_ref, q_row, kv, width, hidden, m_ref, l_ref, a_ref, fresh=True):
    keys, values = kv[:, :HD], kv[:, HD:]
    row = lax.broadcasted_iota(jnp.int32, (SPAN, width), 0)
    col = lax.broadcasted_iota(jnp.int32, (SPAN, width), 1)
    seen = (col - (width - SPAN) <= row) & (col >= hidden)
    for h in range(GROUPS):
        s = score(q_ref[pl.ds(q_row, SPAN), h * HD : (h + 1) * HD], keys)
        s = jnp.where(seen, s, -jnp.inf)
        top = jnp.broadcast_to(jnp.max(s, axis=1, keepdims=True), (SPAN, HD))
        n = i * GROUPS + h
        if not fresh:
            old = m_ref[n]
            top = jnp.maximum(old, top)
            scale = jnp.exp2((old - top) * F32(FACTOR))
        p, total = weigh(s, [top] * (width // HD))
        value = jnp.dot(p, values, preferred_element_type=F32)
        m_ref[n] = top
        l_ref[n] = total if fresh else l_ref[n] * scale + total
        a_ref[n] = value if fresh else a_ref[n] * scale + value


def settle(l_ref, a_ref, o_ref, row):
    for h in range(GROUPS):
        weight = jnp.sum(l_ref[h], axis=1, keepdims=True)
        o_ref[row : row + SPAN, h * HD : (h + 1) * HD] = (a_ref[h] / weight).astype(BF16)


def flash(steps, which, q_ref, chunk_of, shut_of, state, buffers, before=None):
    m_ref, l_ref, a_ref = state
    s_buf, p_buf, f_buf = buffers

    def queries(t, h):
        return q_ref[pl.ds(pl.multiple_of(which(t) * SPAN, SPAN), SPAN), h * HD : (h + 1) * HD]

    def gathered(t, h, half):
        n = which(t) * GROUPS + h
        a_ref[n] = a_ref[n] * f_buf[half] + jnp.dot(
            p_buf[half], chunk_of(t)[:, HD:], preferred_element_type=F32
        )

    p_buf[1] = jnp.zeros(p_buf.shape[1:], p_buf.dtype)
    f_buf[1] = jnp.ones(f_buf.shape[1:], f_buf.dtype)
    s_buf[0] = score(queries(0, 0), chunk_of(0)[:, :HD])

    @pl.loop(0, steps)
    def _(t):
        if before is not None:
            before(t)
        later = jnp.minimum(t + 1, steps - 1)
        shut = shut_of(t)
        for h in range(GROUPS):
            half = h % 2
            if h + 1 < GROUPS:
                s_buf[1 - half] = score(queries(t, h + 1), chunk_of(t)[:, :HD])
            else:
                s_buf[1 - half] = score(queries(later, 0), chunk_of(later)[:, :HD])
            if h:
                gathered(t, h - 1, 1 - half)
            else:
                gathered(jnp.maximum(t - 1, 0), GROUPS - 1, 1)
            s = s_buf[half]
            n = which(t) * GROUPS + h
            old = m_ref[n]
            top = old
            for part in range(CHUNK // SPAN):
                peak = jnp.max(s[:, part * SPAN : (part + 1) * SPAN], axis=1, keepdims=True)
                top = jnp.maximum(top, peak if shut[part] is None else peak - shut[part])
            scale = jnp.exp2((old - top) * F32(FACTOR))
            tops = [top if gone is None else top + gone for gone in shut]
            p, total = weigh(s, [tops[g * HD // SPAN] for g in range(CHUNK // HD)])
            p_buf[half] = p
            f_buf[half] = scale
            m_ref[n] = top
            l_ref[n] = l_ref[n] * scale + total

    gathered(jnp.maximum(steps - 1, 0), GROUPS - 1, 1)


def gather_kernel(
    starts_ref, own_ref, tok_ref, wq_ref, wo_ref, cos_ref, sin_ref, out_ref, w_ref, q_ref, m_ref, l_ref, a_ref,
    tok_buf, wq_buf, kv_buf, s_buf, p_buf, f_buf, kv_sem, send_sem, recv_sem, half_sem, own_sem, tok_sem, wq_sem, ws_sem, wr_sem, wm_sem,
):
    sec = lax.axis_index("sec")
    head = lax.axis_index("head")
    y = sec // 4
    z = (sec // 2) % 2
    c = sec % 2
    x, deep = head % NX, head // NX

    def at(yy, zz, cc):
        return (yy % NY) * 4 + zz * 2 + cc

    up, down = at(y + 1, z, c), at(y + 3, z, c)
    across, mate = at(y, 1 - z, c), at(y, z, 1 - c)
    chunk = tok_buf.shape[1]
    chunks = tok_ref.shape[0] // chunk

    def load(i):
        return pltpu.make_async_copy(
            tok_ref.at[pl.ds(pl.multiple_of(i * chunk, chunk), chunk)],
            tok_buf.at[lax.rem(i, 2)],
            tok_sem.at[lax.rem(i, 2)],
        )

    load_wq = pltpu.make_async_copy(wq_ref, wq_buf, wq_sem)
    load_wq.start()
    load(0).start()
    barrier = pltpu.get_barrier_semaphore()
    for other in (up, down, across, mate):
        pl.semaphore_signal(barrier, inc=1, device_id=(other, head), device_id_type=MESH)
    for r in range(1, NX):
        other = deep * NX + (x + r) % NX
        pl.semaphore_signal(barrier, inc=1, device_id=(sec, other), device_id_type=MESH)
    pl.semaphore_wait(barrier, 3 + NX)

    rows = own_ref.shape[0]
    half = rows // 2
    sent = []

    def push(src, slot, part, target, sem):
        dst = out_ref.at[slot] if part is None else out_ref.at[slot, pl.ds(part * half, half)]
        copy = pltpu.make_async_remote_copy(
            src_ref=src,
            dst_ref=dst,
            send_sem=send_sem.at[len(sent)],
            recv_sem=sem,
            device_id=(target, head),
            device_id_type=MESH,
        )
        copy.start()
        sent.append(copy)

    def relay(slot, target):
        push(out_ref.at[slot], slot, None, target, recv_sem.at[slot])

    def arrived(slot):
        pltpu.make_async_copy(out_ref.at[slot], out_ref.at[slot], recv_sem.at[slot]).wait()

    def half_arrived(slot, part):
        view = out_ref.at[slot, pl.ds(part * half, half)]
        pltpu.make_async_copy(view, view, half_sem.at[part]).wait()

    keep = pltpu.make_async_copy(own_ref, out_ref.at[sec], own_sem)
    keep.start()
    for other in (up, down, across, mate):
        push(own_ref, sec, None, other, recv_sem.at[sec])

    cols = wo_ref.shape[1] // (2 * NX)
    part_rows = pl.ds(c * (wo_ref.shape[0] // 2), wo_ref.shape[0] // 2)

    def give(r, side):
        target = (x + NX - r) % NX
        first = pl.multiple_of(((deep + side) % 2 * NX + target) * cols, cols)
        return pltpu.make_async_remote_copy(
            src_ref=wo_ref.at[part_rows, pl.ds(first, cols)],
            dst_ref=w_ref.at[r - 1, part_rows, pl.ds(side * cols, cols)],
            send_sem=ws_sem.at[r - 1, side],
            recv_sem=wr_sem.at[r - 1, side],
            device_id=(sec, deep * NX + target),
            device_id_type=MESH,
        )

    def share(r):
        view = w_ref.at[r - 1, part_rows]
        return pltpu.make_async_remote_copy(
            src_ref=view,
            dst_ref=view,
            send_sem=wm_sem.at[0, r - 1],
            recv_sem=wm_sem.at[1, r - 1],
            device_id=(mate, head),
            device_id_type=MESH,
        )

    for r in range(1, NX):
        for side in range(2):
            give(r, side).start()

    coarse_rows = cos_ref.shape[0] - FINE
    load_wq.wait()
    @pl.loop(0, chunks)
    def _(i):
        @pl.when(i + 1 < chunks)
        def _():
            load(i + 1).start()

        load(i).wait()
        cos, sin = tile_tables(cos_ref, sin_ref, i * (chunk // FINE), chunk // FINE, coarse_rows)
        q = jnp.dot(tok_buf[lax.rem(i, 2)], wq_buf[...], preferred_element_type=F32)
        lines = pl.ds(pl.multiple_of(i * chunk, chunk), chunk)
        for h in range(GROUPS):
            cut = slice(h * HD, (h + 1) * HD)
            q_ref[lines, cut] = rope(q[:, cut], cos, sin).astype(BF16)

    state, buffers = (m_ref, l_ref, a_ref), (s_buf, p_buf, f_buf)
    blocks = rows // SPAN

    def diagonal(i):
        width = (i + 1) * SPAN
        hidden = starts_ref[sec * blocks + i] - sec * rows
        first_block(i, q_ref, i * SPAN, own_ref[:width, :], width, hidden, *state)

    near = 1 + 2 * (1 - z) * (1 - c)
    steps_back = (4, near, 2, 4 - near)

    def behind(k):
        return (sec + 16 - steps_back[k]) % 16

    def load_kv(k):
        return pltpu.make_async_copy(out_ref.at[behind(k)], kv_buf.at[k % 2], kv_sem.at[k % 2])

    def section(k, first, count):
        def which(t):
            return lax.rem(first + t, EARLY)

        def chunk_of(t):
            start = pl.multiple_of((first + t) // EARLY * CHUNK, CHUNK)
            return kv_buf.at[k % 2, pl.ds(start, CHUNK)]

        def shut_of(t):
            block = (sec - steps_back[k]) * blocks + (first + t) // EARLY * (CHUNK // SPAN)
            low = starts_ref[sec * blocks + which(t)] // SPAN
            out = []
            for part in range(CHUNK // SPAN):
                seen = (block + part >= low) & (block >= 0)
                out.append(jnp.where(seen, F32(0.0), F32(jnp.inf)))
            return out

        flash(count, which, q_ref, chunk_of, shut_of, state, buffers)

    far = at(y + 2, z, c)
    for i in range(blocks // 2):
        diagonal(i)
    arrived(down)
    push(out_ref.at[down, pl.ds(0, half)], down, 0, up, half_sem.at[0])
    relay(down, mate)
    load_kv(0).start()
    arrived(up)
    push(out_ref.at[up, pl.ds(half, half)], up, 1, down, half_sem.at[1])
    relay(up, mate)
    arrived(across)
    relay(across, up)
    relay(across, down)
    relay(across, mate)
    for i in range(blocks // 2, EARLY):
        diagonal(i)
    arrived(behind(1))
    load_kv(1).start()
    load_kv(0).wait()
    section(0, 0, EARLY)
    half_arrived(far, 0)
    half_arrived(far, 1)
    relay(far, across)
    relay(far, mate)
    section(0, EARLY, EARLY)
    load_kv(1).wait()
    section(1, 0, 2 * EARLY)
    for slot in (at(y + 3, 1 - z, c), at(y + 1, 1 - z, c)):
        arrived(slot)
        relay(slot, mate)
    load_kv(2).start()
    for r in range(1, NX):
        for side in range(2):
            give(r, side).wait_recv()
        share(r).start()
    load_kv(2).wait()
    section(2, 0, EARLY)
    slot = at(y + 2, 1 - z, c)
    arrived(slot)
    relay(slot, mate)
    arrived(behind(3))
    load_kv(3).start()
    section(2, EARLY, EARLY)
    load_kv(3).wait()
    section(3, 0, 2 * EARLY)
    for yy in range(NY):
        for zz in range(NZ):
            slot = at(yy, zz, 1 - c)

            @pl.when((slot != behind(1)) & (slot != behind(3)))
            def _():
                arrived(slot)

    view = w_ref.at[0, pl.ds((1 - c) * (wo_ref.shape[0] // 2), wo_ref.shape[0] // 2)]
    for r in range(1, NX):
        pltpu.make_async_copy(view, view, wm_sem.at[1, r - 1]).wait()
    keep.wait()
    for copy in sent:
        copy.wait_send()
    for r in range(1, NX):
        for side in range(2):
            give(r, side).wait_send()
        share(r).wait_send()


def gather(starts, own, tokens, w_query, w_out, tables, sections):
    rows, width = own.shape
    depth, wide = w_query.shape
    hbm = pl.BlockSpec(memory_space=pl.ANY)
    vmem = pl.BlockSpec(memory_space=pltpu.VMEM)
    cols = w_out.shape[1] // NX
    dma = pltpu.SemaphoreType.DMA
    return pl.pallas_call(
        gather_kernel,
        out_shape=(
            jax.ShapeDtypeStruct((sections, rows, width), BF16),
            jax.ShapeDtypeStruct((NX - 1, w_out.shape[0], cols), BF16),
            jax.ShapeDtypeStruct((rows, wide), BF16),
            *[jax.ShapeDtypeStruct((EARLY * GROUPS, SPAN, HD), F32)] * 3,
        ),
        in_specs=[pl.BlockSpec(memory_space=pltpu.SMEM), vmem, hbm, hbm, hbm, vmem, vmem],
        out_specs=(hbm, hbm, vmem, vmem, vmem, vmem),
        scratch_shapes=[
            pltpu.VMEM((2, 256, depth), BF16),
            pltpu.VMEM((depth, wide), BF16),
            pltpu.VMEM((2, rows, width), BF16),
            pltpu.VMEM((2, SPAN, CHUNK), F32),
            pltpu.VMEM((2, SPAN, CHUNK), BF16),
            pltpu.VMEM((2, SPAN, HD), F32),
            dma((2,)),
            dma((16,)),
            dma((16,)),
            dma((2,)),
            dma,
            dma((2,)),
            dma,
            dma((NX - 1, 2)),
            dma((NX - 1, 2)),
            dma((2, NX - 1)),
        ],
        compiler_params=pltpu.CompilerParams(collective_id=0, has_side_effects=True),
        name="gather",
    )(starts, own, tokens, w_query, w_out, *tables)


def attend_kernel(
    starts_ref, q_ref, kv_ref, m_in, l_in, a_in, o_ref, m_out, l_out, a_out, ring, s_buf, p_buf, f_buf, ring_sem, m_ref, l_ref, a_ref
):
    step = pl.program_id(0)
    blocks = pl.num_programs(0)
    section = lax.axis_index("sec")
    low = starts_ref[section * blocks + step] // SPAN
    each = CHUNK // SPAN
    top = jnp.maximum(section - BEHIND, 0) * blocks
    chunks = jnp.maximum(top - low + each - 1, 0) // each

    def fetch(t):
        start = pl.multiple_of((top - (t + 1) * each) * SPAN, SPAN)
        slot = lax.rem(t, NBUF)
        return pltpu.make_async_copy(kv_ref.at[pl.ds(start, CHUNK)], ring.at[slot], ring_sem.at[slot])

    for t in range(NBUF - 2):

        @pl.when(t < chunks)
        def _():
            fetch(t).start()


    @pl.when(step < EARLY)
    def _():
        m_ref[...] = m_in[...]
        l_ref[...] = l_in[...]
        a_ref[...] = a_in[...]

    @pl.when(step >= EARLY)
    def _():
        m_ref[...] = jnp.full(m_ref.shape, -1e30, F32)
        l_ref[...] = jnp.zeros(l_ref.shape, F32)
        a_ref[...] = jnp.zeros(a_ref.shape, F32)

    def chunk_of(t):
        return ring.at[lax.rem(t, NBUF)]

    def shut_of(t):
        block = top - (t + 1) * each
        return [jnp.where(block >= low, F32(0.0), F32(jnp.inf)), None]

    def before(t):
        @pl.when(t + 2 < chunks)
        def _():
            fetch(t + 2).start()

        @pl.when(t + 1 < chunks)
        def _():
            fetch(t + 1).wait()

    @pl.when(chunks > 0)
    def _():
        fetch(0).wait()
        flash(
            chunks, lambda t: 0, q_ref, chunk_of, shut_of, (m_ref, l_ref, a_ref), (s_buf, p_buf, f_buf), before
        )

    @pl.when(step < EARLY)
    def _():
        settle(l_ref, a_ref, o_ref, 0)

    @pl.when(step >= EARLY)
    def _():
        m_out[...] = m_ref[...]
        l_out[...] = l_ref[...]
        a_out[...] = a_ref[...]


def attend(starts, query, kv, state):
    rows, width = query.shape
    pairs = 80
    blocks = rows // SPAN
    state_in = pl.BlockSpec((GROUPS, SPAN, HD), lambda i, s: (jnp.minimum(i, EARLY - 1), 0, 0))
    state_out = pl.BlockSpec((GROUPS, SPAN, HD), lambda i, s: (jnp.maximum(i - EARLY, 0), 0, 0))
    left = jax.ShapeDtypeStruct(((blocks - EARLY) * GROUPS, SPAN, HD), F32)
    return pl.pallas_call(
        attend_kernel,
        out_shape=(jax.ShapeDtypeStruct((EARLY * SPAN, width), BF16), left, left, left),
        grid_spec=pltpu.PrefetchScalarGridSpec(
            num_scalar_prefetch=1,
            grid=(blocks,),
            in_specs=[
                pl.BlockSpec((SPAN, width), lambda i, s: (i, 0)),
                pl.BlockSpec(memory_space=pl.ANY),
                state_in,
                state_in,
                state_in,
            ],
            out_specs=(
                pl.BlockSpec((SPAN, width), lambda i, s: (jnp.minimum(i, EARLY - 1), 0)),
                state_out,
                state_out,
                state_out,
            ),
            scratch_shapes=[
                pltpu.VMEM((NBUF, CHUNK, 2 * HD), BF16),
                pltpu.VMEM((2, SPAN, CHUNK), F32),
                pltpu.VMEM((2, SPAN, CHUNK), BF16),
                pltpu.VMEM((2, SPAN, HD), F32),
                pltpu.SemaphoreType.DMA((NBUF,)),
                *[pltpu.VMEM((GROUPS, SPAN, HD), F32)] * 3,
            ],
        ),
        cost_estimate=pl.CostEstimate(
            flops=pairs * 8 * SPAN * SPAN * HD * GROUPS,
            bytes_accessed=pairs * SPAN * 4 * HD,
            transcendentals=pairs * SPAN * SPAN * GROUPS,
        ),
        name="attend",
    )(starts, query, kv, *state)


def output_kernel(
    starts_ref, early_ref, q_in, kv_in, m_in, l_in, a_in, wo_ref, w_ref, o_ref,
    att_ref, q_ref, kv_ref, m_ref, l_ref, a_ref, s_buf, p_buf, f_buf, in_sem,
    w_buf, near, keep, give, got, w_sem, own_send, own_recv, pass_send, pass_recv, swap_send, swap_recv,
):
    sec = lax.axis_index("sec")
    head = lax.axis_index("head")
    x, deep = head % NX, head // NX
    up = deep * NX + (x + 1) % NX
    down = deep * NX + (x + NX - 1) % NX
    pair = (1 - deep) * NX + x
    count, chunk = own_send.shape[1], give.shape[1]
    half = chunk // 2
    cols = o_ref.shape[1]

    loads = [pltpu.make_async_copy(w_ref.at[r - 1], w_buf.at[r], w_sem.at[r + 1]) for r in range(1, NX)]
    for side in range(2):
        first = pl.multiple_of(((deep + side) % 2 * NX + x) * cols, cols)
        loads.append(
            pltpu.make_async_copy(
                wo_ref.at[:, pl.ds(first, cols)], w_buf.at[0, :, pl.ds(side * cols, cols)], w_sem.at[side]
            )
        )
    rows_early = EARLY * SPAN
    blocks = att_ref.shape[0] // SPAN
    moved = [
        pltpu.make_async_copy(early_ref, att_ref.at[pl.ds(0, rows_early)], in_sem.at[0]),
        pltpu.make_async_copy(q_in.at[pl.ds(rows_early, SPAN)], q_ref, in_sem.at[1]),
        pltpu.make_async_copy(m_in, m_ref, in_sem.at[2]),
        pltpu.make_async_copy(l_in, l_ref, in_sem.at[3]),
        pltpu.make_async_copy(a_in, a_ref, in_sem.at[4]),
    ]
    for k in range(BEHIND + 1):
        moved.append(pltpu.make_async_copy(kv_in.at[(sec + 16 - k) % 16], kv_ref.at[k], in_sem.at[5 + k]))
    for load in moved + loads:
        load.start()
    barrier = pltpu.get_barrier_semaphore()
    for other in (up, down, pair):
        pl.semaphore_signal(barrier, inc=1, device_id=(sec, other), device_id_type=MESH)
    pl.semaphore_wait(barrier, 3)

    def own(way, i):
        rows = pl.ds(pl.multiple_of(i * chunk, chunk), chunk)
        return pltpu.make_async_remote_copy(
            src_ref=att_ref.at[rows],
            dst_ref=near.at[0 if way else 2, rows],
            send_sem=own_send.at[way, i],
            recv_sem=own_recv.at[way, i],
            device_id=(sec, down if way else up),
            device_id_type=MESH,
        )

    def onward(way, i):
        rows = pl.ds(pl.multiple_of(i * chunk + (0 if way else half), half), half)
        return pltpu.make_async_remote_copy(
            src_ref=near.at[0 if way else 2, rows],
            dst_ref=near.at[1, rows],
            send_sem=pass_send.at[way, i],
            recv_sem=pass_recv.at[way, i],
            device_id=(sec, down if way else up),
            device_id_type=MESH,
        )

    def swap(i):
        return pltpu.make_async_remote_copy(
            src_ref=give.at[i],
            dst_ref=got.at[i],
            send_sem=swap_send.at[i],
            recv_sem=swap_recv.at[i],
            device_id=(sec, pair),
            device_id_type=MESH,
        )

    def product(i, side):
        rows = pl.ds(pl.multiple_of(i * chunk, chunk), chunk)
        total = None
        for r in range(NX):
            att = att_ref[rows, :] if r == 0 else near[r - 1, rows, :]
            term = jnp.dot(att, w_buf[r, :, side * cols : (side + 1) * cols], preferred_element_type=F32)
            term = term.astype(BF16).astype(F32)
            total = term if total is None else total + term
        return total

    def launch(i):
        for way in range(2):
            own(way, i).start()

    def relay(i):
        for way in range(2):
            own(way, i).wait_recv()
            onward(way, i).start()

    def finish(j):
        for way in range(2):
            onward(way, j).wait_recv()
        give[j] = product(j, 1).astype(BF16)
        keep[lax.rem(j, 2)] = product(j, 0)
        swap(j).start()

    def add(j):
        swap(j).wait_recv()
        rows = pl.ds(pl.multiple_of(j * chunk, chunk), chunk)
        o_ref[rows, :] = (keep[lax.rem(j, 2)] + got[j].astype(F32)).astype(BF16)

    state, buffers = (m_ref, l_ref, a_ref), (s_buf, p_buf, f_buf)
    block = sec * blocks + EARLY
    low = starts_ref[block]
    per = kv_ref.shape[1] // CHUNK

    def behind(first, steps):
        def chunk_of(t):
            n = first + t
            return kv_ref.at[1 + n // per, pl.ds(pl.multiple_of(lax.rem(n, per) * CHUNK, CHUNK), CHUNK)]

        def shut_of(t):
            n = first + t
            key = (sec - 1 - n // per) * (blocks * SPAN) + lax.rem(n, per) * CHUNK
            return [
                jnp.where((key + part * SPAN >= low) & (key >= 0), F32(0.0), F32(jnp.inf))
                for part in range(CHUNK // SPAN)
            ]

        flash(steps, lambda t: 0, q_ref, chunk_of, shut_of, state, buffers)

    moved[0].wait()
    launch(0)
    launch(1)
    for load in moved[1:]:
        load.wait()
    hidden = low - sec * (blocks * SPAN)
    first_block(0, q_ref, 0, kv_ref.at[0], blocks * SPAN, hidden, *state, fresh=False)
    relay(0)
    launch(2)
    behind(0, BEHIND)
    relay(1)
    launch(3)
    for load in loads:
        load.wait()
    finish(0)
    behind(BEHIND, BEHIND)
    settle(l_ref, a_ref, att_ref, rows_early)

    @pl.loop(2, count + 2)
    def _(i):
        @pl.when(i < count)
        def _():
            relay(i)

        @pl.when(i + 2 < count)
        def _():
            launch(i + 2)

        @pl.when(i <= count)
        def _():
            finish(i - 1)

        add(i - 2)

    @pl.loop(0, count)
    def _(i):
        for way in range(2):
            own(way, i).wait_send()
            onward(way, i).wait_send()
        swap(i).wait_send()


def output(starts, early, query, kv, state, w_out, w_near, chunk=128):
    rows, depth = query.shape
    cols = w_out.shape[1] // (2 * NX)
    count = rows // chunk
    hbm = pl.BlockSpec(memory_space=pl.ANY)
    vmem = pl.BlockSpec(memory_space=pltpu.VMEM)
    dma = pltpu.SemaphoreType.DMA
    return pl.pallas_call(
        output_kernel,
        out_shape=jax.ShapeDtypeStruct((rows, cols), BF16),
        in_specs=[pl.BlockSpec(memory_space=pltpu.SMEM)] + [hbm] * 8,
        out_specs=vmem,
        scratch_shapes=[
            pltpu.VMEM((rows, depth), BF16),
            pltpu.VMEM((SPAN, depth), BF16),
            pltpu.VMEM((BEHIND + 1, *kv.shape[1:]), BF16),
            *[pltpu.VMEM((GROUPS, SPAN, HD), F32)] * 3,
            pltpu.VMEM((2, SPAN, CHUNK), F32),
            pltpu.VMEM((2, SPAN, CHUNK), BF16),
            pltpu.VMEM((2, SPAN, HD), F32),
            dma((6 + BEHIND,)),
            pltpu.VMEM((NX, depth, 2 * cols), BF16),
            pltpu.VMEM((NX - 1, rows, depth), BF16),
            pltpu.VMEM((2, chunk, cols), F32),
            pltpu.VMEM((count, chunk, cols), BF16),
            pltpu.VMEM((count, chunk, cols), BF16),
            dma((NX + 1,)),
            dma((2, count)),
            dma((2, count)),
            dma((2, count)),
            dma((2, count)),
            dma((count,)),
            dma((count,)),
        ],
        compiler_params=pltpu.CompilerParams(collective_id=1, has_side_effects=True),
        name="output",
    )(starts, early, query, kv, *state, w_out, w_near)


def shards(tokens, w_query, w_key, w_value, w_out, key_start):
    rows = tokens.shape[0]
    sections = lax.axis_size("sec")
    section = lax.axis_index("sec")
    tables = rope_tables(section * rows, rows)
    own = project_kv(tokens, w_key, w_value, tables)
    kv, w_near, query, *state = gather(key_start, own, tokens, w_query, w_out, tables, sections)
    early, *state = attend(key_start, query, kv.reshape(sections * rows, 2 * HD), state)
    return output(key_start, early, query, kv, state, w_out, w_near)


def solution(mesh):
    placed = (
        P("sec", None),
        P(None, "head"),
        P(None, "head"),
        P(None, "head"),
        P("head", None),
        P(),
    )
    return jax.shard_map(
        shards, mesh=mesh, in_specs=placed, out_specs=P("sec", "head"), check_vma=False
    )
```
